32 devices in a mesh: depth: 8 (over z, y), lat: 4 (over x, core).
Axes of the slice: x: 2, y: 2, z: 4, core: 2. Of those that a mesh axis runs over, the one named last changes fastest.
Arguments:
- sources: float32 [8, 2, 64, 4096], P('depth', None, None, 'lat'), may hold values from -6 to 6
- down_expand: float32 [8, 2, 64, 4096], P('depth', None, None, 'lat'), may hold values from -0.75 to 0.75
- down_project: float32 [8, 2, 64, 4096], P('depth', None, None, 'lat'), may hold values from -0.09375 to 0.09375
- up_expand: float32 [8, 2, 64, 4096], P('depth', None, None, 'lat'), may hold values from -0.75 to 0.75
- up_project: float32 [8, 2, 64, 4096], P('depth', None, None, 'lat'), may hold values from -0.09375 to 0.09375
- down_decay: float32 [8, 64], P('depth'), may hold values from 0.3 to 0.8
- up_decay: float32 [8, 64], P('depth'), may hold values from 0.3 to 0.8
- active_list: int32 [8, 64], P('depth'), may hold values from 0 to 63, each once within a row
- active_count: int32 [8], P('depth'), may hold values from 1 to 64
- incident_down: float32 [2, 64, 4096], P(None, None, 'lat'), may hold values from -6 to 6
- incident_up: float32 [2, 64, 4096], P(None, None, 'lat'), may hold values from -6 to 6
Outputs:
- field: float32 [8, 2, 64, 4096], P('depth', None, None, 'lat')
The draws below stay inside these ranges and needn't reach their ends.
Inputs may be any that keep to these rules, and one draw needn't show every extreme that they name: Each row of active_list holds every source number once.
All inputs are finite; a program needn't handle non-finite values.
Results may differ from the reference program's by a relative error of at most 0.0003.
Values sent between devices are 32-bit elements; how exact they have to be, the bound alone decides.
No kernel may reach another device: no remote copies, remote signals or barrier semaphores. Data moves between devices by JAX's collectives and lax.ppermute only.
A program may use at most 64 MiB of HBM per device.

```python
import math
import jax
import jax.numpy as jnp
from jax import lax

SRC = 64
RANK = 64
LAT = 4096
GROUPS = 8


def plant(entries, rng, low, largest):
    longest = entries.shape.index(max(entries.shape))
    spots = []
    for shift in (0, 1):
        where = [jax.random.randint(jax.random.fold_in(rng, axis), (), 0, length) for axis, length in enumerate(entries.shape)]
        where[longest] = (where[longest] + shift) % entries.shape[longest]
        spots.append(tuple(where))
    return entries.at[spots[0]].set(low).at[spots[1]].set(largest)


def shard_levels(key, shape, cuts, low, top_value):
    loudness, own = 1.0, jax.random.fold_in(key, 6)
    for axis_at, parts in cuts:
        heights = jnp.exp(jax.random.uniform(jax.random.fold_in(own, axis_at), (parts,), jnp.float32, low / len(cuts), top_value / len(cuts)))
        loudness = loudness * jnp.repeat(heights, shape[axis_at] // parts).reshape([-1 if axis == axis_at else 1 for axis in range(len(shape))])
    return loudness


def gaussian(own_key, shape, deviation, limit, shards=(), held_as=jnp.bfloat16):
    gain = shard_levels(own_key, shape, shards, -0.22, 0.18) if shards else 1.0
    array = jax.random.normal(own_key, shape, jnp.float32) * deviation * gain
    return jnp.minimum(jnp.maximum(array, -limit), limit).astype(held_as)


def setup_inputs(seed: int = 0) -> dict:
    key_list = jax.random.split(jax.random.key(seed), 12)
    return {
        "sources": gaussian(key_list[0], (GROUPS, 2, SRC, LAT), 1.0, 6.0, ((0, 8), (3, 4)), jnp.float32),
        "down_expand": gaussian(key_list[1], (GROUPS, 2, RANK, LAT), RANK ** -0.5, 0.75, ((0, 8), (3, 4)), jnp.float32),
        "down_project": gaussian(key_list[2], (GROUPS, 2, RANK, LAT), LAT ** -0.5, 0.09375, ((0, 8), (3, 4)), jnp.float32),
        "up_expand": gaussian(key_list[3], (GROUPS, 2, RANK, LAT), RANK ** -0.5, 0.75, ((0, 8), (3, 4)), jnp.float32),
        "up_project": gaussian(key_list[4], (GROUPS, 2, RANK, LAT), LAT ** -0.5, 0.09375, ((0, 8), (3, 4)), jnp.float32),
        "down_decay": jnp.clip(jnp.exp(math.log(0.8) - 0.98082923 * jax.random.uniform(key_list[5], (GROUPS, RANK), jnp.float32) ** shard_levels(key_list[5], (GROUPS, RANK), ((0, 8),), -0.2, 0.2)), 0.3, 0.8),
        "up_decay": jnp.clip(jnp.exp(math.log(0.8) - 0.98082923 * jax.random.uniform(key_list[6], (GROUPS, RANK), jnp.float32) ** shard_levels(key_list[6], (GROUPS, RANK), ((0, 8),), -0.2, 0.2)), 0.3, 0.8),
        "active_list": jax.vmap(lambda own: jax.random.permutation(own, SRC))(jax.random.split(key_list[7], GROUPS)).reshape((GROUPS, SRC)).astype(jnp.int32),
        "active_count": plant(jax.random.randint(key_list[8], (GROUPS,), 1, SRC + 1), jax.random.fold_in(key_list[8], 1), 1, SRC).astype(jnp.int32),
        "incident_down": gaussian(key_list[9], (2, SRC, LAT), 1.0, 6.0, ((2, 4),), jnp.float32),
        "incident_up": gaussian(key_list[10], (2, SRC, LAT), 1.0, 6.0, ((2, 4),), jnp.float32),
    }


def contract(left, right):
    hp = lax.Precision.HIGHEST
    dims = (((1,), (1,)), ((), ()))
    def prod(a, b):
        return lax.dot_general(a, b, dims, precision=hp, preferred_element_type=jnp.float32)
    real = prod(left[0], right[0]) - prod(left[1], right[1])
    imag = prod(left[0], right[1]) + prod(left[1], right[0])
    return jnp.stack([real, imag])


def expand(coef, basis):
    hp = lax.Precision.HIGHEST
    dims = (((0,), (0,)), ((), ()))
    def prod(a, b):
        return lax.dot_general(a, b, dims, precision=hp, preferred_element_type=jnp.float32)
    real = prod(coef[0], basis[0]) - prod(coef[1], basis[1])
    imag = prod(coef[0], basis[1]) + prod(coef[1], basis[0])
    return jnp.stack([real, imag])


def reference(sources, down_expand, down_project, up_expand, up_project, down_decay, up_decay, active_list, active_count, incident_down, incident_up):
    places = jnp.arange(SRC, dtype=jnp.int32)
    valid = (places[None, :] < active_count[:, None]).astype(jnp.float32)
    hits = (active_list[:, :, None] == places[None, None, :]).astype(jnp.float32)
    mask = jnp.sum(valid[:, :, None] * hits, axis=1)
    local = sources * mask[:, None, :, None]

    def sweep(prev, items):
        wave, proj, basis, decay = items
        coef = decay[None, :, None] * contract(proj, prev)
        term = expand(coef, basis)
        return wave + term, term

    _, down_terms = lax.scan(sweep, incident_down, (local, down_project, down_expand, down_decay))
    _, up_terms = lax.scan(sweep, incident_up, (local, up_project, up_expand, up_decay), reverse=True)
    return local + down_terms + up_terms
```

```python
import jax
import jax.numpy as jnp
from jax import lax
from jax.experimental import pallas as pl
from jax.experimental.pallas import tpu as pltpu
from jax.sharding import PartitionSpec as P

F32 = jnp.float32
BF16 = jnp.bfloat16
VMEM = pl.BlockSpec(memory_space=pltpu.VMEM)
SMEM = pl.BlockSpec(memory_space=pltpu.SMEM)


def split(value):
    high = value.astype(BF16)
    return high, (value - high.astype(F32)).astype(BF16)


def dot3(left, right, dims):
    def prod(a, b):
        return lax.dot_general(a, b, (dims, ((), ())), preferred_element_type=F32)

    return prod(left[0], right[0]) + (prod(left[0], right[1]) + prod(left[1], right[0]))


ROWS_COLS = ((1,), (0,))
ROWS_ROWS = ((1,), (1,))


def turned(value):
    half = value.shape[1] // 2
    lanes = lax.broadcasted_iota(jnp.int32, value.shape, 1)
    swapped = pltpu.roll(value, half, 1)
    return jnp.where(lanes < half, -swapped, swapped)


def joined(product):
    half = product.shape[0] // 2
    return product[:half] + turned(product[half:])


def spread(rows):
    half = rows.shape[1] // 2
    lanes = lax.broadcasted_iota(jnp.int32, rows.shape, 1)
    return jnp.concatenate([jnp.where(lanes < half, rows, -rows), pltpu.roll(rows, half, 1)], axis=0)


def apply_map(rows, step):
    rank = step.shape[1] // 2
    matrix = step[:rank]
    full = jnp.concatenate([matrix, turned(matrix)], axis=0)
    return dot3(split(rows), split(full), ROWS_COLS)


def compose(later, earlier):
    rank = later.shape[1] // 2
    out = apply_map(earlier, later)
    return jnp.concatenate([out[:rank], out[rank:] + later[rank:]], axis=0)


def advance(step, rows):
    rank = step.shape[1] // 2
    return apply_map(rows, step) + step[rank:]


def entry_kernel(dp_ref, up_ref, di_ref, ui_ref, out_ref):
    for k, (proj, wave) in enumerate(((dp_ref, di_ref), (up_ref, ui_ref))):
        half = wave.shape[0] // 2
        out = dot3(split(wave[...]), split(proj[...]), ROWS_ROWS)
        out_ref[k * half : (k + 1) * half] = joined(out)


def prepare_kernel(edge_ref, count_ref, list_ref, src_ref, de_ref, ue_ref, dd_ref, ud_ref, entry_ref, loc_ref, left_ref):
    nsrc = src_ref.shape[0] // 2
    rank = de_ref.shape[0] // 2
    rows = lax.broadcasted_iota(jnp.int32, (nsrc, list_ref.shape[1]), 0)
    cols = lax.broadcasted_iota(jnp.int32, (nsrc, list_ref.shape[1]), 1)
    hit = (rows == list_ref[...]) & (cols < count_ref[0])
    mask = jnp.sum(jnp.where(hit, 1.0, 0.0), axis=1, keepdims=True)
    local = src_ref[...] * jnp.concatenate([mask, mask], axis=0)
    loc_ref[...] = local
    eye = lax.broadcasted_iota(jnp.int32, (rank, rank), 0) == lax.broadcasted_iota(jnp.int32, (rank, rank), 1)
    for k, (basis_ref, decay_ref) in enumerate(((de_ref, dd_ref), (ue_ref, ud_ref))):
        decay = jnp.sum(jnp.where(eye, decay_ref[...], 0.0), axis=1, keepdims=True)
        basis = split(basis_ref[...] * jnp.concatenate([decay, decay], axis=0))
        first = jnp.where(edge_ref[k] == 1, entry_ref[k * nsrc : (k + 1) * nsrc], 0.0)
        trace = split(local + dot3(split(spread(first)), basis, ROWS_COLS))
        for part in (0, 1):
            left_ref[k, part, : 2 * rank] = basis[part]
            left_ref[k, part, 2 * rank :] = trace[part]


def gram_kernel(which, proj_ref, left_ref, out_ref):
    rank = proj_ref.shape[0] // 2
    out = dot3((left_ref[which, 0], left_ref[which, 1]), split(proj_ref[...]), ROWS_ROWS)
    half = out.shape[0] // 2
    out_ref[:rank] = joined(out[: 2 * rank])
    out_ref[rank:] = joined(out[2 * rank :])


def pair_kernel(flag_ref, own_ref, other_ref, near_ref, out_ref):
    own, other = own_ref[...], other_ref[...]
    first = flag_ref[0] == 0
    near = jnp.where(first, own, other)
    far = jnp.where(first, other, own)
    near_ref[...] = near
    out_ref[...] = compose(far, near)


def total_kernel(flag_ref, own_ref, other_ref, out_ref):
    own, other = own_ref[...], other_ref[...]
    lower = flag_ref[0] == 0
    out_ref[...] = compose(jnp.where(lower, other, own), jnp.where(lower, own, other))


def total_offset_kernel(flag_ref, own_ref, other_ref, out_ref):
    own, other = own_ref[...], other_ref[...]
    rank = own.shape[1] // 2
    lower = flag_ref[0] == 0
    out_ref[...] = advance(jnp.where(lower, other, own), jnp.where(lower, own, other)[rank:])


def final_kernel(flags_ref, carry_ref, gap_ref, near_ref, entry_ref, out_ref):
    nsrc = carry_ref.shape[0]
    carry = carry_ref[...]
    carry = jnp.where(flags_ref[0] == 1, advance(gap_ref[...], carry), carry)
    carry = jnp.where(flags_ref[1] == 1, advance(near_ref[...], carry), carry)
    entry = jnp.where(flags_ref[3] == 0, entry_ref[:nsrc], entry_ref[nsrc:])
    out_ref[...] = jnp.where(flags_ref[2] == 1, entry, carry)


def expand_kernel(role_ref, own_ref, other_ref, left_ref, loc_ref, out_ref):
    rank2 = own_ref.shape[1]
    total = loc_ref[...]
    for role, rows_ref in ((role_ref[0], own_ref), (1 - role_ref[0], other_ref)):
        basis = (left_ref[role, 0, :rank2], left_ref[role, 1, :rank2])
        total = total + dot3(split(spread(rows_ref[...])), basis, ROWS_COLS)
    out_ref[...] = total


def call(kernel, outs, *args, scalars=0):
    return pl.pallas_call(
        kernel,
        out_shape=outs,
        in_specs=[SMEM] * scalars + [VMEM] * (len(args) - scalars),
        out_specs=jax.tree.map(lambda _: VMEM, outs),
    )(*args)


def shape(*dims, dtype=F32):
    return jax.ShapeDtypeStruct(dims, dtype)


def body(
    sources,
    down_expand,
    down_project,
    up_expand,
    up_project,
    down_decay,
    up_decay,
    active_list,
    active_count,
    incident_down,
    incident_up,
):
    nsrc, width = sources.shape[2:]
    rank = down_expand.shape[2]
    depth, lat = lax.axis_size("depth"), lax.axis_size("lat")
    group = lax.axis_index("depth")
    role = lax.rem(lax.axis_index("lat"), 2)
    place = jnp.where(role == 0, group, depth - 1 - group)
    pair = place // 2

    def flat(value):
        return value.reshape(value.shape[-3] * value.shape[-2], value.shape[-1])

    def flags(*values):
        return jnp.stack([jnp.asarray(value).astype(jnp.int32) for value in values])

    def shifted(value, step):
        pairs = [(k, k + step) for k in range(depth) if 0 <= k + step < depth]
        return lax.ppermute(value, "depth", pairs)

    def swapped(value, axis, bit):
        return lax.ppermute(value, axis, [(k, k ^ bit) for k in range(lax.axis_size(axis))])

    ahead = shifted(flat(down_project), -1)
    behind = shifted(flat(up_project), 1)

    entry = call(entry_kernel, shape(2 * nsrc, 2 * rank), flat(down_project), flat(up_project), flat(incident_down), flat(incident_up))
    bit = 1
    while bit < lat:
        entry = entry + swapped(entry, "lat", bit)
        bit *= 2
    local, left = call(
        prepare_kernel,
        (shape(2 * nsrc, width), shape(2, 2, 2 * rank + 2 * nsrc, width, dtype=BF16)),
        flags(group == 0, group == depth - 1),
        active_count,
        active_list,
        flat(sources),
        flat(down_expand),
        flat(up_expand),
        down_decay,
        up_decay,
        entry,
        scalars=2,
    )
    element = shape(rank + nsrc, 2 * rank)

    def gram(which, proj):
        return call(lambda *refs: gram_kernel(which, *refs), element, proj, left)

    down, up = gram(0, ahead), gram(1, behind)
    own = jnp.where(role == 0, down, up) + swapped(jnp.where(role == 0, up, down), "lat", 1)
    bit = 2
    while bit < lat:
        own = own + swapped(own, "lat", bit)
        bit *= 2

    near, total = call(pair_kernel, (element, element), flags(lax.rem(place, 2)), own, swapped(own, "depth", 1), scalars=1)

    gap, has_gap = near, jnp.int32(0)
    reach = 2
    while reach < depth // 2:
        upper = (place // reach) % 2
        other = swapped(total, "depth", reach)
        if reach == 2:
            gap, has_gap = other, upper
        else:
            joint = call(lambda _, a, b, o: total_kernel(_, a, b, o), element, flags(1), gap, other, scalars=1)
            gap = jnp.where(upper == 1, jnp.where(has_gap == 1, joint, other), gap)
            has_gap = jnp.maximum(has_gap, upper)
        last = reach * 2 >= depth // 2
        kernel = total_offset_kernel if last else total_kernel
        total = call(kernel, shape(nsrc, 2 * rank) if last else element, flags(upper), total, other, scalars=1)
        reach *= 2
    half = depth // 2
    moves = []
    for k in range(half):
        for j in range(lat):
            low, high = (k, k + half) if j % 2 == 0 else (depth - 1 - k, half - 1 - k)
            moves.append((low * lat + j, high * lat + j))
    carry = lax.ppermute(total, ("depth", "lat"), moves)
    coef = call(
        final_kernel,
        shape(nsrc, 2 * rank),
        flags(has_gap, lax.rem(place, 2), place == 0, role),
        carry,
        gap,
        near,
        entry,
        scalars=1,
    )
    field = call(expand_kernel, shape(2 * nsrc, width), flags(role), coef, swapped(coef, "lat", 1), left, local, scalars=1)
    return field.reshape(sources.shape)


def solution(mesh):
    in_specs = (
        P("depth", None, None, "lat"),
        P("depth", None, None, "lat"),
        P("depth", None, None, "lat"),
        P("depth", None, None, "lat"),
        P("depth", None, None, "lat"),
        P("depth", None),
        P("depth", None),
        P("depth", None),
        P("depth"),
        P(None, None, "lat"),
        P(None, None, "lat"),
    )
    out_specs = P("depth", None, None, "lat")
    return jax.shard_map(body, mesh=mesh, in_specs=in_specs, out_specs=out_specs, check_vma=False)
```

```python
import functools

import jax
import jax.numpy as jnp
from jax import lax
from jax.experimental import pallas as pl
from jax.experimental.pallas import tpu as pltpu
from jax.sharding import PartitionSpec as P

F32 = jnp.float32
BF16 = jnp.bfloat16
VMEM = pl.BlockSpec(memory_space=pltpu.VMEM)
SMEM = pl.BlockSpec(memory_space=pltpu.SMEM)


def split(value):
    high = value.astype(BF16)
    return high, (value - high.astype(F32)).astype(BF16)


def dot3(left, right, dims):
    def prod(a, b):
        return lax.dot_general(a, b, (dims, ((), ())), preferred_element_type=F32)

    return prod(left[0], right[0]) + (prod(left[0], right[1]) + prod(left[1], right[0]))


ROWS_COLS = ((1,), (0,))
ROWS_ROWS = ((1,), (1,))


def turned(value):
    half = value.shape[1] // 2
    lanes = lax.broadcasted_iota(jnp.int32, value.shape, 1)
    swapped = pltpu.roll(value, half, 1)
    return jnp.where(lanes < half, -swapped, swapped)


def joined(product):
    half = product.shape[0] // 2
    return product[:half] + turned(product[half:])


def spread(rows):
    half = rows.shape[1] // 2
    lanes = lax.broadcasted_iota(jnp.int32, rows.shape, 1)
    return jnp.concatenate([jnp.where(lanes < half, rows, -rows), pltpu.roll(rows, half, 1)], axis=0)


def apply_map(rows, step):
    rank = step.shape[1] // 2
    matrix = step[:rank]
    full = jnp.concatenate([matrix, turned(matrix)], axis=0)
    return dot3(split(rows), split(full), ROWS_COLS)


def compose(later, earlier):
    rank = later.shape[1] // 2
    out = apply_map(earlier, later)
    return jnp.concatenate([out[:rank], out[rank:] + later[rank:]], axis=0)


def advance(step, rows):
    rank = step.shape[1] // 2
    return apply_map(rows, step) + step[rank:]


def standing():
    group, depth = lax.axis_index("depth"), lax.axis_size("depth")
    role = lax.rem(lax.axis_index("lat"), 2)
    return role, jnp.where(role == 0, group, depth - 1 - group)


def entry_kernel(dp_ref, up_ref, di_ref, ui_ref, out_ref):
    for k, (proj, wave) in enumerate(((dp_ref, di_ref), (up_ref, ui_ref))):
        half = wave.shape[0] // 2
        out = dot3(split(wave[...]), split(proj[...]), ROWS_ROWS)
        out_ref[k * half : (k + 1) * half] = joined(out)


def prepare_kernel(count_ref, list_ref, src_ref, de_ref, ue_ref, dd_ref, ud_ref, entry_ref, loc_ref, left_ref):
    group, depth = lax.axis_index("depth"), lax.axis_size("depth")
    nsrc = src_ref.shape[0] // 2
    rank = de_ref.shape[0] // 2
    rows = lax.broadcasted_iota(jnp.int32, (nsrc, list_ref.shape[1]), 0)
    cols = lax.broadcasted_iota(jnp.int32, (nsrc, list_ref.shape[1]), 1)
    hit = (rows == list_ref[...]) & (cols < count_ref[0])
    mask = jnp.sum(jnp.where(hit, 1.0, 0.0), axis=1, keepdims=True)
    local = src_ref[...] * jnp.concatenate([mask, mask], axis=0)
    loc_ref[...] = local
    eye = lax.broadcasted_iota(jnp.int32, (rank, rank), 0) == lax.broadcasted_iota(jnp.int32, (rank, rank), 1)
    for k, (basis_ref, decay_ref, edge) in enumerate(((de_ref, dd_ref, 0), (ue_ref, ud_ref, depth - 1))):
        decay = jnp.sum(jnp.where(eye, decay_ref[...], 0.0), axis=1, keepdims=True)
        basis = split(basis_ref[...] * jnp.concatenate([decay, decay], axis=0))
        first = jnp.where(group == edge, entry_ref[k * nsrc : (k + 1) * nsrc], 0.0)
        trace = split(local + dot3(split(spread(first)), basis, ROWS_COLS))
        for part in (0, 1):
            left_ref[k, part, : 2 * rank] = basis[part]
            left_ref[k, part, 2 * rank :] = trace[part]


def gram_kernel(which, proj_ref, left_ref, out_ref):
    rank = proj_ref.shape[0] // 2
    out = dot3((left_ref[which, 0], left_ref[which, 1]), split(proj_ref[...]), ROWS_ROWS)
    out_ref[:rank] = joined(out[: 2 * rank])
    out_ref[rank:] = joined(out[2 * rank :])


def pair_kernel(own_ref, other_ref, near_ref, out_ref):
    place = standing()[1]
    own, other = own_ref[...], other_ref[...]
    first = lax.rem(place, 2) == 0
    near = jnp.where(first, own, other)
    near_ref[...] = near
    out_ref[...] = compose(jnp.where(first, other, own), near)


def ordered(reach, own_ref, other_ref):
    own, other = own_ref[...], other_ref[...]
    lower = lax.rem(lax.div(standing()[1], reach), 2) == 0
    return jnp.where(lower, own, other), jnp.where(lower, other, own)


def total_kernel(reach, own_ref, other_ref, out_ref):
    earlier, later = ordered(reach, own_ref, other_ref)
    out_ref[...] = compose(later, earlier)


def total_offset_kernel(reach, own_ref, other_ref, out_ref):
    earlier, later = ordered(reach, own_ref, other_ref)
    out_ref[...] = advance(later, earlier[earlier.shape[1] // 2 :])


def gap_kernel(reach, own_ref, other_ref, out_ref):
    place = standing()[1]
    own, other = own_ref[...], other_ref[...]
    started = lax.rem(place, reach) >= 2
    upper = lax.rem(lax.div(place, reach), 2) == 1
    longer = jnp.where(started, compose(own, other), other)
    out_ref[...] = jnp.where(upper, longer, own)


def final_kernel(carry_ref, gap_ref, near_ref, entry_ref, out_ref):
    depth = lax.axis_size("depth")
    role, place = standing()
    nsrc = carry_ref.shape[0]
    carry = carry_ref[...]
    carry = jnp.where(lax.rem(place, depth // 2) >= 2, advance(gap_ref[...], carry), carry)
    carry = jnp.where(lax.rem(place, 2) == 1, advance(near_ref[...], carry), carry)
    entry = jnp.where(role == 0, entry_ref[:nsrc], entry_ref[nsrc:])
    out_ref[...] = jnp.where(place == 0, entry, carry)


def expand_kernel(turn, rows_ref, left_ref, sum_ref, out_ref):
    role = lax.rem(standing()[0] + turn, 2)
    wide = rows_ref.shape[1]
    basis = (left_ref[role, 0, :wide], left_ref[role, 1, :wide])
    out_ref[...] = sum_ref[...] + dot3(split(spread(rows_ref[...])), basis, ROWS_COLS)


def call(kernel, outs, *args, scalars=0, grant=4):
    return pl.pallas_call(
        kernel,
        out_shape=outs,
        in_specs=[SMEM] * scalars + [VMEM] * (len(args) - scalars),
        out_specs=jax.tree.map(lambda _: VMEM, outs),
        compiler_params=pltpu.CompilerParams(vmem_limit_bytes=grant << 20),
    )(*args)


def shape(*dims, dtype=F32):
    return jax.ShapeDtypeStruct(dims, dtype)


def body(
    sources,
    down_expand,
    down_project,
    up_expand,
    up_project,
    down_decay,
    up_decay,
    active_list,
    active_count,
    incident_down,
    incident_up,
):
    nsrc, width = sources.shape[2:]
    rank = down_expand.shape[2]
    depth, lat = lax.axis_size("depth"), lax.axis_size("lat")
    role = lax.rem(lax.axis_index("lat"), 2)
    element = shape(rank + nsrc, 2 * rank)

    def flat(value):
        return value.reshape(value.shape[-3] * value.shape[-2], value.shape[-1])

    def shifted(value, step):
        pairs = [(k, k + step) for k in range(depth) if 0 <= k + step < depth]
        return lax.ppermute(value, "depth", pairs)

    def swapped(value, axis, bit):
        return lax.ppermute(value, axis, [(k, k ^ bit) for k in range(lax.axis_size(axis))])

    ahead = shifted(flat(down_project), -1)
    behind = shifted(flat(up_project), 1)

    entry = call(
        entry_kernel,
        shape(2 * nsrc, 2 * rank),
        flat(down_project),
        flat(up_project),
        flat(incident_down),
        flat(incident_up),
        grant=12,
    )
    bit = 1
    while bit < lat:
        entry = entry + swapped(entry, "lat", bit)
        bit *= 2
    local, left = call(
        prepare_kernel,
        (shape(2 * nsrc, width), shape(2, 2, 2 * rank + 2 * nsrc, width, dtype=BF16)),
        active_count,
        active_list,
        flat(sources),
        flat(down_expand),
        flat(up_expand),
        down_decay,
        up_decay,
        entry,
        scalars=1,
        grant=12,
    )

    def gram(which, proj):
        return call(functools.partial(gram_kernel, which), element, proj, left)

    down, up = gram(0, ahead), gram(1, behind)
    own = jnp.where(role == 0, down, up) + swapped(jnp.where(role == 0, up, down), "lat", 1)
    bit = 2
    while bit < lat:
        own = own + swapped(own, "lat", bit)
        bit *= 2

    near, total = call(pair_kernel, (element, element), own, swapped(own, "depth", 1))
    gap = near
    reach = 2
    while reach < depth // 2:
        other = swapped(total, "depth", reach)
        gap = other if reach == 2 else call(functools.partial(gap_kernel, reach), element, gap, other)
        last = reach * 2 >= depth // 2
        kernel = functools.partial(total_offset_kernel if last else total_kernel, reach)
        total = call(kernel, shape(nsrc, 2 * rank) if last else element, total, other)
        reach *= 2
    half = depth // 2
    moves = []
    for k in range(half):
        for j in range(lat):
            low, high = (k, k + half) if j % 2 == 0 else (depth - 1 - k, half - 1 - k)
            moves.append((low * lat + j, high * lat + j))
    carry = lax.ppermute(total, ("depth", "lat"), moves)
    coef = call(final_kernel, shape(nsrc, 2 * rank), carry, gap, near, entry)
    wide = shape(2 * nsrc, width)
    field = call(functools.partial(expand_kernel, 0), wide, coef, left, local)
    field = call(functools.partial(expand_kernel, 1), wide, swapped(coef, "lat", 1), left, field)
    return field.reshape(sources.shape)


def solution(mesh):
    in_specs = (
        P("depth", None, None, "lat"),
        P("depth", None, None, "lat"),
        P("depth", None, None, "lat"),
        P("depth", None, None, "lat"),
        P("depth", None, None, "lat"),
        P("depth", None),
        P("depth", None),
        P("depth", None),
        P("depth"),
        P(None, None, "lat"),
        P(None, None, "lat"),
    )
    out_specs = P("depth", None, None, "lat")
    return jax.shard_map(body, mesh=mesh, in_specs=in_specs, out_specs=out_specs, check_vma=False)
```

```python
import functools

import jax
import jax.numpy as jnp
from jax import lax
from jax.experimental import pallas as pl
from jax.experimental.pallas import tpu as pltpu
from jax.sharding import PartitionSpec as P

F32 = jnp.float32
BF16 = jnp.bfloat16
VMEM = pl.BlockSpec(memory_space=pltpu.VMEM)
SMEM = pl.BlockSpec(memory_space=pltpu.SMEM)


def split(value):
    high = value.astype(BF16)
    return high, (value - high.astype(F32)).astype(BF16)


def dot3(left, right, dims):
    def prod(a, b):
        return lax.dot_general(a, b, (dims, ((), ())), preferred_element_type=F32)

    return prod(left[0], right[0]) + (prod(left[0], right[1]) + prod(left[1], right[0]))


ROWS_COLS = ((1,), (0,))
ROWS_ROWS = ((1,), (1,))


def turned(value):
    half = value.shape[1] // 2
    lanes = lax.broadcasted_iota(jnp.int32, value.shape, 1)
    swapped = pltpu.roll(value, half, 1)
    return jnp.where(lanes < half, -swapped, swapped)


def joined(product):
    half = product.shape[0] // 2
    return product[:half] + turned(product[half:])


def spread(rows):
    half = rows.shape[1] // 2
    lanes = lax.broadcasted_iota(jnp.int32, rows.shape, 1)
    return jnp.concatenate([jnp.where(lanes < half, rows, -rows), pltpu.roll(rows, half, 1)], axis=0)


def apply_map(rows, step):
    rank = step.shape[1] // 2
    matrix = step[:rank]
    full = jnp.concatenate([matrix, turned(matrix)], axis=0)
    return dot3(split(rows), split(full), ROWS_COLS)


def compose(later, earlier):
    rank = later.shape[1] // 2
    out = apply_map(earlier, later)
    return jnp.concatenate([out[:rank], out[rank:] + later[rank:]], axis=0)


def advance(step, rows):
    rank = step.shape[1] // 2
    return apply_map(rows, step) + step[rank:]


def standing():
    group, depth = lax.axis_index("depth"), lax.axis_size("depth")
    role = lax.rem(lax.axis_index("lat"), 2)
    return role, jnp.where(role == 0, group, depth - 1 - group)


def entry_kernel(dp_ref, up_ref, di_ref, ui_ref, out_ref):
    for k, (proj, wave) in enumerate(((dp_ref, di_ref), (up_ref, ui_ref))):
        half = wave.shape[0] // 2
        out = dot3(split(wave[...]), split(proj[...]), ROWS_ROWS)
        out_ref[k * half : (k + 1) * half] = joined(out)


def prepare_kernel(count_ref, list_ref, src_ref, de_ref, ue_ref, dd_ref, ud_ref, entry_ref, loc_ref, left_ref):
    group, depth = lax.axis_index("depth"), lax.axis_size("depth")
    nsrc = src_ref.shape[0] // 2
    rank = de_ref.shape[0] // 2
    rows = lax.broadcasted_iota(jnp.int32, (nsrc, list_ref.shape[1]), 0)
    cols = lax.broadcasted_iota(jnp.int32, (nsrc, list_ref.shape[1]), 1)
    hit = (rows == list_ref[...]) & (cols < count_ref[0])
    mask = jnp.sum(jnp.where(hit, 1.0, 0.0), axis=1, keepdims=True)
    local = src_ref[...] * jnp.concatenate([mask, mask], axis=0)
    loc_ref[...] = local
    eye = lax.broadcasted_iota(jnp.int32, (rank, rank), 0) == lax.broadcasted_iota(jnp.int32, (rank, rank), 1)
    for k, (basis_ref, decay_ref, edge) in enumerate(((de_ref, dd_ref, 0), (ue_ref, ud_ref, depth - 1))):
        decay = jnp.sum(jnp.where(eye, decay_ref[...], 0.0), axis=1, keepdims=True)
        basis = split(basis_ref[...] * jnp.concatenate([decay, decay], axis=0))
        first = jnp.where(group == edge, entry_ref[k * nsrc : (k + 1) * nsrc], 0.0)
        trace = split(local + dot3(split(spread(first)), basis, ROWS_COLS))
        for part in (0, 1):
            left_ref[k, part, : 2 * rank] = basis[part]
            left_ref[k, part, 2 * rank :] = trace[part]


def gram_kernel(which, proj_ref, left_ref, out_ref):
    rank = proj_ref.shape[0] // 2
    out = dot3((left_ref[which, 0], left_ref[which, 1]), split(proj_ref[...]), ROWS_ROWS)
    out_ref[:rank] = joined(out[: 2 * rank])
    out_ref[rank:] = joined(out[2 * rank :])


def pair_kernel(own_ref, other_ref, near_ref, out_ref):
    place = standing()[1]
    own, other = own_ref[...], other_ref[...]
    first = lax.rem(place, 2) == 0
    near = jnp.where(first, own, other)
    near_ref[...] = near
    out_ref[...] = compose(jnp.where(first, other, own), near)


def ordered(reach, own_ref, other_ref):
    own, other = own_ref[...], other_ref[...]
    lower = lax.rem(lax.div(standing()[1], reach), 2) == 0
    return jnp.where(lower, own, other), jnp.where(lower, other, own)


def total_kernel(reach, own_ref, other_ref, out_ref):
    earlier, later = ordered(reach, own_ref, other_ref)
    out_ref[...] = compose(later, earlier)


def total_offset_kernel(reach, own_ref, other_ref, out_ref):
    earlier, later = ordered(reach, own_ref, other_ref)
    out_ref[...] = advance(later, earlier[earlier.shape[1] // 2 :])


def gap_kernel(reach, own_ref, other_ref, out_ref):
    place = standing()[1]
    own, other = own_ref[...], other_ref[...]
    started = lax.rem(place, reach) >= 2
    upper = lax.rem(lax.div(place, reach), 2) == 1
    longer = jnp.where(started, compose(own, other), other)
    out_ref[...] = jnp.where(upper, longer, own)


def prefix_kernel(half, near_ref, gap_ref, out_ref):
    place = standing()[1]
    near, gap = near_ref[...], gap_ref[...]
    odd = lax.rem(place, 2) == 1
    both = jnp.where(odd, compose(near, gap), gap)
    out_ref[...] = jnp.where(lax.rem(place, half) >= 2, both, near)


def final_kernel(half, carry_ref, prefix_ref, entry_ref, out_ref):
    role, place = standing()
    nsrc = carry_ref.shape[0]
    carry = jnp.where(place >= half, carry_ref[...], 0.0)
    carry = jnp.where(lax.rem(place, half) > 0, advance(prefix_ref[...], carry), carry)
    entry = jnp.where(role == 0, entry_ref[:nsrc], entry_ref[nsrc:])
    out_ref[...] = jnp.where(place == 0, entry, carry)


def expanded(turn, rows_ref, left_ref, sum_ref, columns):
    role = lax.rem(standing()[0] + turn, 2)
    wide = rows_ref.shape[1]
    basis = (left_ref[role, 0, :wide, columns], left_ref[role, 1, :wide, columns])
    return sum_ref[:, columns] + dot3(split(spread(rows_ref[...])), basis, ROWS_COLS)


def expand_kernel(rows_ref, left_ref, sum_ref, out_ref):
    out_ref[...] = expanded(0, rows_ref, left_ref, sum_ref, slice(None))


def finish_kernel(rows_ref, left_ref, sum_ref, out_ref, held_ref, done):
    chunks = done.shape[0]
    width = held_ref.shape[1] // chunks
    copies = []
    for k in range(chunks):
        columns = slice(k * width, (k + 1) * width)
        held_ref[:, columns] = expanded(1, rows_ref, left_ref, sum_ref, columns)
        copies.append(pltpu.make_async_copy(held_ref.at[:, columns], out_ref.at[:, columns], done.at[k]))
        copies[-1].start()
    for copy in copies:
        copy.wait()


def call(kernel, outs, *args, scalars=0, grant=4):
    return pl.pallas_call(
        kernel,
        out_shape=outs,
        in_specs=[SMEM] * scalars + [VMEM] * (len(args) - scalars),
        out_specs=jax.tree.map(lambda _: VMEM, outs),
        compiler_params=pltpu.CompilerParams(vmem_limit_bytes=grant << 20),
    )(*args)


def shape(*dims, dtype=F32):
    return jax.ShapeDtypeStruct(dims, dtype)


def body(
    sources,
    down_expand,
    down_project,
    up_expand,
    up_project,
    down_decay,
    up_decay,
    active_list,
    active_count,
    incident_down,
    incident_up,
):
    nsrc, width = sources.shape[2:]
    rank = down_expand.shape[2]
    depth, lat = lax.axis_size("depth"), lax.axis_size("lat")
    role = lax.rem(lax.axis_index("lat"), 2)
    element = shape(rank + nsrc, 2 * rank)

    def flat(value):
        return value.reshape(value.shape[-3] * value.shape[-2], value.shape[-1])

    def shifted(value, step):
        return lax.ppermute(value, "depth", [(k, (k + step) % depth) for k in range(depth)])

    def swapped(value, axis, bit):
        return lax.ppermute(value, axis, [(k, k ^ bit) for k in range(lax.axis_size(axis))])

    ahead = shifted(flat(down_project), -1)
    behind = shifted(flat(up_project), 1)

    entry = call(
        entry_kernel,
        shape(2 * nsrc, 2 * rank),
        flat(down_project),
        flat(up_project),
        flat(incident_down),
        flat(incident_up),
        grant=12,
    )
    bit = 1
    while bit < lat:
        entry = entry + swapped(entry, "lat", bit)
        bit *= 2
    local, left = call(
        prepare_kernel,
        (shape(2 * nsrc, width), shape(2, 2, 2 * rank + 2 * nsrc, width, dtype=BF16)),
        active_count,
        active_list,
        flat(sources),
        flat(down_expand),
        flat(up_expand),
        down_decay,
        up_decay,
        entry,
        scalars=1,
        grant=12,
    )

    def gram(which, proj):
        return call(functools.partial(gram_kernel, which), element, proj, left)

    down, up = gram(0, ahead), gram(1, behind)
    own = jnp.where(role == 0, down, up) + swapped(jnp.where(role == 0, up, down), "lat", 1)
    bit = 4
    while bit < lat:
        own = own + swapped(own, "lat", bit)
        bit *= 2
    other = swapped(own, "depth", 1)
    if lat > 2:
        across = [(g * lat + j, (g ^ 1) * lat + (j ^ 2)) for g in range(depth) for j in range(lat)]
        other = other + lax.ppermute(own, ("depth", "lat"), across)
        own = own + swapped(own, "lat", 2)

    near, total = call(pair_kernel, (element, element), own, other)
    gap = near
    reach, half = 2, depth // 2
    while reach < half:
        other = swapped(total, "depth", reach)
        gap = other if reach == 2 else call(functools.partial(gap_kernel, reach), element, gap, other)
        last = reach * 2 >= half
        kernel = functools.partial(total_offset_kernel if last else total_kernel, reach)
        total = call(kernel, shape(nsrc, 2 * rank) if last else element, total, other)
        reach *= 2
    carry = swapped(total, "depth", half)
    prefix = call(functools.partial(prefix_kernel, half), element, near, gap)
    coef = call(functools.partial(final_kernel, half), shape(nsrc, 2 * rank), carry, prefix, entry)
    wide = shape(2 * nsrc, width)
    field = call(expand_kernel, wide, coef, left, local)
    chunks = 4
    field = pl.pallas_call(
        finish_kernel,
        out_shape=wide,
        in_specs=[VMEM] * 3,
        out_specs=pl.BlockSpec(memory_space=pl.ANY),
        scratch_shapes=[pltpu.VMEM(wide.shape, F32), pltpu.SemaphoreType.DMA((chunks,))],
        compiler_params=pltpu.CompilerParams(vmem_limit_bytes=4 << 20),
    )(swapped(coef, "lat", 1), left, field)
    return field.reshape(sources.shape)


def solution(mesh):
    in_specs = (
        P("depth", None, None, "lat"),
        P("depth", None, None, "lat"),
        P("depth", None, None, "lat"),
        P("depth", None, None, "lat"),
        P("depth", None, None, "lat"),
        P("depth", None),
        P("depth", None),
        P("depth", None),
        P("depth"),
        P(None, None, "lat"),
        P(None, None, "lat"),
    )
    out_specs = P("depth", None, None, "lat")
    return jax.shard_map(body, mesh=mesh, in_specs=in_specs, out_specs=out_specs, check_vma=False)
```

```python
import functools

import jax
import jax.numpy as jnp
from jax import lax
from jax.experimental import pallas as pl
from jax.experimental.pallas import tpu as pltpu
from jax.sharding import PartitionSpec as P

F32 = jnp.float32
BF16 = jnp.bfloat16
VMEM = pl.BlockSpec(memory_space=pltpu.VMEM)
SMEM = pl.BlockSpec(memory_space=pltpu.SMEM)


def split(value):
    high = value.astype(BF16)
    return high, (value - high.astype(F32)).astype(BF16)


ROWS_COLS = ((1,), (0,))
ROWS_ROWS = ((1,), (1,))


def dot3(left, right, dims):
    def prod(a, b):
        return lax.dot_general(a, b, (dims, ((), ())), preferred_element_type=F32)

    if dims == ROWS_COLS:
        return prod(jnp.concatenate([left[0], left[0], left[1]], 1), jnp.concatenate([right[0], right[1], right[0]], 0))
    count = right[0].shape[0]
    both = prod(left[0], jnp.concatenate(right, 0))
    return both[:, :count] + (both[:, count:] + prod(left[1], right[0]))


def turned(value):
    half = value.shape[1] // 2
    lanes = lax.broadcasted_iota(jnp.int32, value.shape, 1)
    swapped = pltpu.roll(value, half, 1)
    return jnp.where(lanes < half, -swapped, swapped)


def joined(product):
    half = product.shape[0] // 2
    return product[:half] + turned(product[half:])


def spread(rows):
    half = rows.shape[1] // 2
    lanes = lax.broadcasted_iota(jnp.int32, rows.shape, 1)
    return jnp.concatenate([jnp.where(lanes < half, rows, -rows), pltpu.roll(rows, half, 1)], axis=0)


def apply_map(rows, step):
    rank = step.shape[1] // 2
    matrix = step[:rank]
    full = jnp.concatenate([matrix, turned(matrix)], axis=0)
    return dot3(split(rows), split(full), ROWS_COLS)


def compose(later, earlier):
    rank = later.shape[1] // 2
    out = apply_map(earlier, later)
    return jnp.concatenate([out[:rank], out[rank:] + later[rank:]], axis=0)


def advance(step, rows):
    rank = step.shape[1] // 2
    return apply_map(rows, step) + step[rank:]


def parity(value):
    odd = value & 1
    for bit in range(1, 16):
        odd = odd ^ ((value >> bit) & 1)
    return odd


def standing():
    group, depth = lax.axis_index("depth"), lax.axis_size("depth")
    role = parity(group ^ lax.axis_index("lat"))
    return role, jnp.where(role == 0, group, depth - 1 - group)


def entry_kernel(dp_ref, up_ref, di_ref, ui_ref, out_ref):
    for k, (proj, wave) in enumerate(((dp_ref, di_ref), (up_ref, ui_ref))):
        half = wave.shape[0] // 2
        out = dot3(split(wave[...]), split(proj[...]), ROWS_ROWS)
        out_ref[k * half : (k + 1) * half] = joined(out)


def prepare_kernel(count_ref, list_ref, src_ref, de_ref, ue_ref, dd_ref, ud_ref, entry_ref, loc_ref, left_ref):
    group, depth = lax.axis_index("depth"), lax.axis_size("depth")
    nsrc = src_ref.shape[0] // 2
    rank = de_ref.shape[0] // 2
    rows = lax.broadcasted_iota(jnp.int32, (nsrc, list_ref.shape[1]), 0)
    cols = lax.broadcasted_iota(jnp.int32, (nsrc, list_ref.shape[1]), 1)
    hit = (rows == list_ref[...]) & (cols < count_ref[0])
    mask = jnp.sum(jnp.where(hit, 1.0, 0.0), axis=1, keepdims=True)
    local = src_ref[...] * jnp.concatenate([mask, mask], axis=0)
    loc_ref[...] = local
    eye = lax.broadcasted_iota(jnp.int32, (rank, rank), 0) == lax.broadcasted_iota(jnp.int32, (rank, rank), 1)
    for k, (basis_ref, decay_ref, edge) in enumerate(((de_ref, dd_ref, 0), (ue_ref, ud_ref, depth - 1))):
        decay = jnp.sum(jnp.where(eye, decay_ref[...], 0.0), axis=1, keepdims=True)
        basis = split(basis_ref[...] * jnp.concatenate([decay, decay], axis=0))
        first = jnp.where(group == edge, entry_ref[k * nsrc : (k + 1) * nsrc], 0.0)
        trace = split(local + dot3(split(spread(first)), basis, ROWS_COLS))
        for part in (0, 1):
            left_ref[k, part, : 2 * rank] = basis[part]
            left_ref[k, part, 2 * rank :] = trace[part]


def gram_kernel(which, proj_ref, left_ref, out_ref):
    rank = proj_ref.shape[0] // 2
    out = dot3((left_ref[which, 0], left_ref[which, 1]), split(proj_ref[...]), ROWS_ROWS)
    out_ref[:rank] = joined(out[: 2 * rank])
    out_ref[rank:] = joined(out[2 * rank :])


def pair_kernel(own_ref, other_ref, near_ref, out_ref):
    place = standing()[1]
    own, other = own_ref[...], other_ref[...]
    first = lax.rem(place, 2) == 0
    near = jnp.where(first, own, other)
    near_ref[...] = near
    out_ref[...] = compose(jnp.where(first, other, own), near)


def ordered(reach, own_ref, other_ref):
    own, other = own_ref[...], other_ref[...]
    lower = lax.rem(lax.div(standing()[1], reach), 2) == 0
    return jnp.where(lower, own, other), jnp.where(lower, other, own)


def total_kernel(reach, own_ref, other_ref, out_ref):
    earlier, later = ordered(reach, own_ref, other_ref)
    out_ref[...] = compose(later, earlier)


def total_offset_kernel(reach, own_ref, other_ref, out_ref):
    earlier, later = ordered(reach, own_ref, other_ref)
    out_ref[...] = advance(later, earlier[earlier.shape[1] // 2 :])


def gap_kernel(reach, own_ref, other_ref, out_ref):
    place = standing()[1]
    own, other = own_ref[...], other_ref[...]
    started = lax.rem(place, reach) >= 2
    upper = lax.rem(lax.div(place, reach), 2) == 1
    longer = jnp.where(started, compose(own, other), other)
    out_ref[...] = jnp.where(upper, longer, own)


def prefix_kernel(half, near_ref, gap_ref, out_ref):
    place = standing()[1]
    near, gap = near_ref[...], gap_ref[...]
    odd = lax.rem(place, 2) == 1
    both = jnp.where(odd, compose(near, gap), gap)
    out_ref[...] = jnp.where(lax.rem(place, half) >= 2, both, near)


def final_kernel(half, carry_ref, prefix_ref, entry_ref, out_ref):
    role, place = standing()
    nsrc = carry_ref.shape[0]
    carry = jnp.where(place >= half, carry_ref[...], 0.0)
    carry = jnp.where(lax.rem(place, half) > 0, advance(prefix_ref[...], carry), carry)
    entry = jnp.where(role == 0, entry_ref[:nsrc], entry_ref[nsrc:])
    out_ref[...] = jnp.where(place == 0, entry, carry)


def expanded(turn, rows_ref, left_ref, sum_ref, columns):
    role = lax.rem(standing()[0] + turn, 2)
    wide = rows_ref.shape[1]
    basis = (left_ref[role, 0, :wide, columns], left_ref[role, 1, :wide, columns])
    return sum_ref[:, columns] + dot3(split(spread(rows_ref[...])), basis, ROWS_COLS)


def expand_kernel(rows_ref, left_ref, sum_ref, out_ref):
    out_ref[...] = expanded(0, rows_ref, left_ref, sum_ref, slice(None))


def finish_kernel(rows_ref, left_ref, sum_ref, out_ref, held_ref, done):
    chunks = done.shape[0]
    width = held_ref.shape[1] // chunks
    copies = []
    for k in range(chunks):
        columns = slice(k * width, (k + 1) * width)
        held_ref[:, columns] = expanded(1, rows_ref, left_ref, sum_ref, columns)
        copies.append(pltpu.make_async_copy(held_ref.at[:, columns], out_ref.at[:, columns], done.at[k]))
        copies[-1].start()
    for copy in copies:
        copy.wait()


def call(kernel, outs, *args, scalars=0, grant=4):
    return pl.pallas_call(
        kernel,
        out_shape=outs,
        in_specs=[SMEM] * scalars + [VMEM] * (len(args) - scalars),
        out_specs=jax.tree.map(lambda _: VMEM, outs),
        compiler_params=pltpu.CompilerParams(vmem_limit_bytes=grant << 20),
    )(*args)


def shape(*dims, dtype=F32):
    return jax.ShapeDtypeStruct(dims, dtype)


def body(
    sources,
    down_expand,
    down_project,
    up_expand,
    up_project,
    down_decay,
    up_decay,
    active_list,
    active_count,
    incident_down,
    incident_up,
):
    nsrc, width = sources.shape[2:]
    rank = down_expand.shape[2]
    depth, lat = lax.axis_size("depth"), lax.axis_size("lat")
    role = standing()[0]
    element = shape(rank + nsrc, 2 * rank)

    def flat(value):
        return value.reshape(value.shape[-3] * value.shape[-2], value.shape[-1])

    def shifted(value, step):
        return lax.ppermute(value, "depth", [(k, (k + step) % depth) for k in range(depth)])

    def swapped(value, deep, wide):
        pairs = [(g * lat + j, (g ^ deep) * lat + (j ^ wide)) for g in range(depth) for j in range(lat)]
        return lax.ppermute(value, ("depth", "lat"), pairs)

    def met(value, deep, wide):
        return swapped(value, deep, wide ^ parity(deep ^ wide))

    ahead = shifted(flat(down_project), -1)
    behind = shifted(flat(up_project), 1)

    entry = call(
        entry_kernel,
        shape(2 * nsrc, 2 * rank),
        flat(down_project),
        flat(up_project),
        flat(incident_down),
        flat(incident_up),
        grant=12,
    )
    bit = 1
    while bit < lat:
        entry = entry + swapped(entry, 0, bit)
        bit *= 2
    local, left = call(
        prepare_kernel,
        (shape(2 * nsrc, width), shape(2, 2, 2 * rank + 2 * nsrc, width, dtype=BF16)),
        active_count,
        active_list,
        flat(sources),
        flat(down_expand),
        flat(up_expand),
        down_decay,
        up_decay,
        entry,
        scalars=1,
        grant=12,
    )

    def gram(which, proj):
        return call(functools.partial(gram_kernel, which), element, proj, left)

    down, up = gram(0, ahead), gram(1, behind)
    own = jnp.where(role == 0, down, up) + swapped(jnp.where(role == 0, up, down), 0, 1)
    bit = 4
    while bit < lat:
        own = own + met(own, 0, bit)
        bit *= 2
    other = met(own, 1, 0)
    if lat > 2:
        other = other + met(own, 1, 2)
        own = own + met(own, 0, 2)

    near, total = call(pair_kernel, (element, element), own, other)
    gap = near
    reach, half = 2, depth // 2
    while reach < half:
        other = met(total, reach, 0)
        gap = other if reach == 2 else call(functools.partial(gap_kernel, reach), element, gap, other)
        last = reach * 2 >= half
        kernel = functools.partial(total_offset_kernel if last else total_kernel, reach)
        total = call(kernel, shape(nsrc, 2 * rank) if last else element, total, other)
        reach *= 2
    carry = met(total, half, 0)
    prefix = call(functools.partial(prefix_kernel, half), element, near, gap)
    coef = call(functools.partial(final_kernel, half), shape(nsrc, 2 * rank), carry, prefix, entry)
    wide = shape(2 * nsrc, width)
    field = call(expand_kernel, wide, coef, left, local)
    chunks = 4
    field = pl.pallas_call(
        finish_kernel,
        out_shape=wide,
        in_specs=[VMEM] * 3,
        out_specs=pl.BlockSpec(memory_space=pl.ANY),
        scratch_shapes=[pltpu.VMEM(wide.shape, F32), pltpu.SemaphoreType.DMA((chunks,))],
        compiler_params=pltpu.CompilerParams(vmem_limit_bytes=4 << 20),
    )(swapped(coef, 0, 1), left, field)
    return field.reshape(sources.shape)


def solution(mesh):
    in_specs = (
        P("depth", None, None, "lat"),
        P("depth", None, None, "lat"),
        P("depth", None, None, "lat"),
        P("depth", None, None, "lat"),
        P("depth", None, None, "lat"),
        P("depth", None),
        P("depth", None),
        P("depth", None),
        P("depth"),
        P(None, None, "lat"),
        P(None, None, "lat"),
    )
    out_specs = P("depth", None, None, "lat")
    return jax.shard_map(body, mesh=mesh, in_specs=in_specs, out_specs=out_specs, check_vma=False)
```

```python
import functools

import jax
import jax.numpy as jnp
from jax import lax
from jax.experimental import pallas as pl
from jax.experimental.pallas import tpu as pltpu
from jax.sharding import PartitionSpec as P

F32 = jnp.float32
BF16 = jnp.bfloat16
VMEM = pl.BlockSpec(memory_space=pltpu.VMEM)
SMEM = pl.BlockSpec(memory_space=pltpu.SMEM)


def split(value):
    high = value.astype(BF16)
    return high, (value - high.astype(F32)).astype(BF16)


ROWS_COLS = ((1,), (0,))
ROWS_ROWS = ((1,), (1,))


def dot3(left, right, dims):
    def prod(a, b):
        return lax.dot_general(a, b, (dims, ((), ())), preferred_element_type=F32)

    if dims == ROWS_COLS:
        return prod(jnp.concatenate([left[0], left[0], left[1]], 1), jnp.concatenate([right[0], right[1], right[0]], 0))
    count = right[0].shape[0]
    both = prod(left[0], jnp.concatenate(right, 0))
    return both[:, :count] + (both[:, count:] + prod(left[1], right[0]))


def turned(value):
    half = value.shape[1] // 2
    lanes = lax.broadcasted_iota(jnp.int32, value.shape, 1)
    swapped = pltpu.roll(value, half, 1)
    return jnp.where(lanes < half, -swapped, swapped)


def joined(product):
    half = product.shape[0] // 2
    return product[:half] + turned(product[half:])


def spread(rows):
    half = rows.shape[1] // 2
    lanes = lax.broadcasted_iota(jnp.int32, rows.shape, 1)
    return jnp.concatenate([jnp.where(lanes < half, rows, -rows), pltpu.roll(rows, half, 1)], axis=0)


def apply_map(rows, step):
    rank = step.shape[1] // 2
    matrix = step[:rank]
    full = jnp.concatenate([matrix, turned(matrix)], axis=0)
    return dot3(split(rows), split(full), ROWS_COLS)


def compose(later, earlier):
    rank = later.shape[1] // 2
    out = apply_map(earlier, later)
    return jnp.concatenate([out[:rank], out[rank:] + later[rank:]], axis=0)


def advance(step, rows):
    rank = step.shape[1] // 2
    return apply_map(rows, step) + step[rank:]


def parity(value):
    odd = value & 1
    for bit in range(1, 16):
        odd = odd ^ ((value >> bit) & 1)
    return odd


def standing():
    group, depth = lax.axis_index("depth"), lax.axis_size("depth")
    role = parity(group ^ lax.axis_index("lat"))
    return role, jnp.where(role == 0, group, depth - 1 - group)


def entry_kernel(dp_ref, up_ref, di_ref, ui_ref, out_ref):
    for k, (proj, wave) in enumerate(((dp_ref, di_ref), (up_ref, ui_ref))):
        half = wave.shape[0] // 2
        out = dot3(split(wave[...]), split(proj[...]), ROWS_ROWS)
        out_ref[k * half : (k + 1) * half] = joined(out)


def prepare_kernel(count_ref, list_ref, src_ref, de_ref, ue_ref, dd_ref, ud_ref, entry_ref, loc_ref, left_ref):
    group, depth = lax.axis_index("depth"), lax.axis_size("depth")
    nsrc = src_ref.shape[0] // 2
    rank = de_ref.shape[0] // 2
    rows = lax.broadcasted_iota(jnp.int32, (nsrc, list_ref.shape[1]), 0)
    cols = lax.broadcasted_iota(jnp.int32, (nsrc, list_ref.shape[1]), 1)
    hit = (rows == list_ref[...]) & (cols < count_ref[0])
    mask = jnp.sum(jnp.where(hit, 1.0, 0.0), axis=1, keepdims=True)
    local = src_ref[...] * jnp.concatenate([mask, mask], axis=0)
    loc_ref[...] = local
    eye = lax.broadcasted_iota(jnp.int32, (rank, rank), 0) == lax.broadcasted_iota(jnp.int32, (rank, rank), 1)
    for k, (basis_ref, decay_ref, edge) in enumerate(((de_ref, dd_ref, 0), (ue_ref, ud_ref, depth - 1))):
        decay = jnp.sum(jnp.where(eye, decay_ref[...], 0.0), axis=1, keepdims=True)
        basis = split(basis_ref[...] * jnp.concatenate([decay, decay], axis=0))
        first = jnp.where(group == edge, entry_ref[k * nsrc : (k + 1) * nsrc], 0.0)
        trace = split(local + dot3(split(spread(first)), basis, ROWS_COLS))
        for part in (0, 1):
            left_ref[k, part, : 2 * rank] = basis[part]
            left_ref[k, part, 2 * rank :] = trace[part]


def gram(which, proj_ref, left_ref):
    rank = proj_ref.shape[0] // 2
    out = dot3((left_ref[which, 0], left_ref[which, 1]), split(proj_ref[...]), ROWS_ROWS)
    return jnp.concatenate([joined(out[: 2 * rank]), joined(out[2 * rank :])], 0)


def first_gram_kernel(proj_ref, left_ref, out_ref):
    out_ref[...] = gram(1, proj_ref, left_ref)


def second_gram_kernel(proj_ref, left_ref, first_ref, keep_ref, give_ref):
    down, up = gram(0, proj_ref, left_ref), first_ref[...]
    ours = standing()[0] == 0
    keep_ref[...] = jnp.where(ours, down, up)
    give_ref[...] = jnp.where(ours, up, down)


def pair_kernel(count, *refs):
    parts, (near_ref, out_ref) = refs[:-2], refs[-2:]
    other = sum((ref[...] for ref in parts[1:count]), parts[0][...])
    own = sum((ref[...] for ref in parts[count + 1 :]), parts[count][...])
    first = lax.rem(standing()[1], 2) == 0
    near = jnp.where(first, own, other)
    near_ref[...] = near
    out_ref[...] = compose(jnp.where(first, other, own), near)


def ordered(reach, own_ref, other_ref):
    own, other = own_ref[...], other_ref[...]
    lower = lax.rem(lax.div(standing()[1], reach), 2) == 0
    return jnp.where(lower, own, other), jnp.where(lower, other, own)


def total_kernel(reach, own_ref, other_ref, out_ref):
    earlier, later = ordered(reach, own_ref, other_ref)
    out_ref[...] = compose(later, earlier)


def total_offset_kernel(reach, own_ref, other_ref, out_ref):
    earlier, later = ordered(reach, own_ref, other_ref)
    out_ref[...] = advance(later, earlier[earlier.shape[1] // 2 :])


def gap_kernel(reach, own_ref, other_ref, out_ref):
    place = standing()[1]
    own, other = own_ref[...], other_ref[...]
    started = lax.rem(place, reach) >= 2
    upper = lax.rem(lax.div(place, reach), 2) == 1
    longer = jnp.where(started, compose(own, other), other)
    out_ref[...] = jnp.where(upper, longer, own)


def prefix_kernel(half, near_ref, gap_ref, out_ref):
    place = standing()[1]
    near, gap = near_ref[...], gap_ref[...]
    odd = lax.rem(place, 2) == 1
    both = jnp.where(odd, compose(near, gap), gap)
    out_ref[...] = jnp.where(lax.rem(place, half) >= 2, both, near)


def final_kernel(half, carry_ref, prefix_ref, entry_ref, out_ref):
    role, place = standing()
    nsrc = carry_ref.shape[0]
    carry = jnp.where(place >= half, carry_ref[...], 0.0)
    carry = jnp.where(lax.rem(place, half) > 0, advance(prefix_ref[...], carry), carry)
    entry = jnp.where(role == 0, entry_ref[:nsrc], entry_ref[nsrc:])
    out_ref[...] = jnp.where(place == 0, entry, carry)


def expanded(turn, rows_ref, left_ref, sum_ref, columns):
    role = lax.rem(standing()[0] + turn, 2)
    wide = rows_ref.shape[1]
    basis = (left_ref[role, 0, :wide, columns], left_ref[role, 1, :wide, columns])
    return sum_ref[:, columns] + dot3(split(spread(rows_ref[...])), basis, ROWS_COLS)


def expand_kernel(rows_ref, left_ref, sum_ref, out_ref):
    out_ref[...] = expanded(0, rows_ref, left_ref, sum_ref, slice(None))


def finish_kernel(rows_ref, left_ref, sum_ref, out_ref, held_ref, done):
    width = held_ref.shape[1]
    copies = []
    for k, (start, stop) in enumerate(((0, width // 4), (width // 4, width))):
        columns = slice(start, stop)
        held_ref[:, columns] = expanded(1, rows_ref, left_ref, sum_ref, columns)
        copies.append(pltpu.make_async_copy(held_ref.at[:, columns], out_ref.at[:, columns], done.at[k]))
        copies[-1].start()
    for copy in copies:
        copy.wait()


def call(kernel, outs, *args, scalars=0, grant=4):
    return pl.pallas_call(
        kernel,
        out_shape=outs,
        in_specs=[SMEM] * scalars + [VMEM] * (len(args) - scalars),
        out_specs=jax.tree.map(lambda _: VMEM, outs),
        compiler_params=pltpu.CompilerParams(vmem_limit_bytes=grant << 20),
    )(*args)


def shape(*dims, dtype=F32):
    return jax.ShapeDtypeStruct(dims, dtype)


def body(
    sources,
    down_expand,
    down_project,
    up_expand,
    up_project,
    down_decay,
    up_decay,
    active_list,
    active_count,
    incident_down,
    incident_up,
):
    nsrc, width = sources.shape[2:]
    rank = down_expand.shape[2]
    depth, lat = lax.axis_size("depth"), lax.axis_size("lat")
    element = shape(rank + nsrc, 2 * rank)

    def flat(value):
        return value.reshape(value.shape[-3] * value.shape[-2], value.shape[-1])

    def shifted(value, step):
        return lax.ppermute(value, "depth", [(k, (k + step) % depth) for k in range(depth)])

    def swapped(value, deep, wide):
        pairs = [(g * lat + j, (g ^ deep) * lat + (j ^ wide)) for g in range(depth) for j in range(lat)]
        return lax.ppermute(value, ("depth", "lat"), pairs)

    def met(value, deep, wide):
        return swapped(value, deep, wide ^ parity(deep ^ wide))

    ahead = shifted(flat(down_project), -1)
    behind = shifted(flat(up_project), 1)

    entry = call(
        entry_kernel,
        shape(2 * nsrc, 2 * rank),
        flat(down_project),
        flat(up_project),
        flat(incident_down),
        flat(incident_up),
        grant=12,
    )
    bit = 1
    while bit < lat:
        entry = entry + swapped(entry, 0, bit)
        bit *= 2
    local, left = call(
        prepare_kernel,
        (shape(2 * nsrc, width), shape(2, 2, 2 * rank + 2 * nsrc, width, dtype=BF16)),
        active_count,
        active_list,
        flat(sources),
        flat(down_expand),
        flat(up_expand),
        down_decay,
        up_decay,
        entry,
        scalars=1,
        grant=12,
    )

    first = call(first_gram_kernel, element, behind, left)
    keep, give = call(second_gram_kernel, (element, element), ahead, left, first)
    own = keep + swapped(give, 0, 1)
    bit = 4
    while bit < lat:
        own = own + met(own, 0, bit)
        bit *= 2
    owns, others = [own], []
    if lat > 2:
        others.append(met(own, 1, 2))
        owns.append(met(own, 0, 2))
    others.append(met(own, 1, 0))

    near, total = call(functools.partial(pair_kernel, len(others)), (element, element), *others, *owns)
    gap = near
    reach, half = 2, depth // 2
    while reach < half:
        other = met(total, reach, 0)
        gap = other if reach == 2 else call(functools.partial(gap_kernel, reach), element, gap, other)
        last = reach * 2 >= half
        kernel = functools.partial(total_offset_kernel if last else total_kernel, reach)
        total = call(kernel, shape(nsrc, 2 * rank) if last else element, total, other)
        reach *= 2
    carry = met(total, half, 0)
    prefix = call(functools.partial(prefix_kernel, half), element, near, gap)
    coef = call(functools.partial(final_kernel, half), shape(nsrc, 2 * rank), carry, prefix, entry)
    wide = shape(2 * nsrc, width)
    field = call(expand_kernel, wide, coef, left, local)
    field = pl.pallas_call(
        finish_kernel,
        out_shape=wide,
        in_specs=[VMEM] * 3,
        out_specs=pl.BlockSpec(memory_space=pl.ANY),
        scratch_shapes=[pltpu.VMEM(wide.shape, F32), pltpu.SemaphoreType.DMA((2,))],
        compiler_params=pltpu.CompilerParams(vmem_limit_bytes=4 << 20),
    )(swapped(coef, 0, 1), left, field)
    return field.reshape(sources.shape)


def solution(mesh):
    in_specs = (
        P("depth", None, None, "lat"),
        P("depth", None, None, "lat"),
        P("depth", None, None, "lat"),
        P("depth", None, None, "lat"),
        P("depth", None, None, "lat"),
        P("depth", None),
        P("depth", None),
        P("depth", None),
        P("depth"),
        P(None, None, "lat"),
        P(None, None, "lat"),
    )
    out_specs = P("depth", None, None, "lat")
    return jax.shard_map(body, mesh=mesh, in_specs=in_specs, out_specs=out_specs, check_vma=False)
```

```python
import functools

import jax
import jax.numpy as jnp
from jax import lax
from jax.experimental import pallas as pl
from jax.experimental.pallas import tpu as pltpu
from jax.sharding import PartitionSpec as P

F32 = jnp.float32
BF16 = jnp.bfloat16
VMEM = pl.BlockSpec(memory_space=pltpu.VMEM)
SMEM = pl.BlockSpec(memory_space=pltpu.SMEM)


def split(value):
    high = value.astype(BF16)
    return high, (value - high.astype(F32)).astype(BF16)


ROWS_COLS = ((1,), (0,))
ROWS_ROWS = ((1,), (1,))


def dot3(left, right, dims):
    def prod(a, b):
        return lax.dot_general(a, b, (dims, ((), ())), preferred_element_type=F32)

    if dims == ROWS_COLS:
        return prod(jnp.concatenate([left[0], left[0], left[1]], 1), jnp.concatenate([right[0], right[1], right[0]], 0))
    count = right[0].shape[0]
    both = prod(left[0], jnp.concatenate(right, 0))
    return both[:, :count] + (both[:, count:] + prod(left[1], right[0]))


def turned(value):
    half = value.shape[1] // 2
    lanes = lax.broadcasted_iota(jnp.int32, value.shape, 1)
    swapped = pltpu.roll(value, half, 1)
    return jnp.where(lanes < half, -swapped, swapped)


def joined(product):
    half = product.shape[0] // 2
    return product[:half] + turned(product[half:])


def spread(rows):
    half = rows.shape[1] // 2
    lanes = lax.broadcasted_iota(jnp.int32, rows.shape, 1)
    return jnp.concatenate([jnp.where(lanes < half, rows, -rows), pltpu.roll(rows, half, 1)], axis=0)


def apply_map(rows, step):
    rank = step.shape[1] // 2
    matrix = step[:rank]
    full = jnp.concatenate([matrix, turned(matrix)], axis=0)
    return dot3(split(rows), split(full), ROWS_COLS)


def compose(later, earlier):
    rank = later.shape[1] // 2
    out = apply_map(earlier, later)
    return jnp.concatenate([out[:rank], out[rank:] + later[rank:]], axis=0)


def advance(step, rows):
    rank = step.shape[1] // 2
    return apply_map(rows, step) + step[rank:]


def parity(value):
    odd = value & 1
    for bit in range(1, 16):
        odd = odd ^ ((value >> bit) & 1)
    return odd


def standing():
    group, depth = lax.axis_index("depth"), lax.axis_size("depth")
    role = parity(group ^ lax.axis_index("lat"))
    return role, jnp.where(role == 0, group, depth - 1 - group)


def entry_kernel(dp_ref, up_ref, di_ref, ui_ref, out_ref):
    for k, (proj, wave) in enumerate(((dp_ref, di_ref), (up_ref, ui_ref))):
        half = wave.shape[0] // 2
        out = dot3(split(wave[...]), split(proj[...]), ROWS_ROWS)
        out_ref[k * half : (k + 1) * half] = joined(out)


def prepare_kernel(count_ref, list_ref, src_ref, de_ref, ue_ref, dd_ref, ud_ref, entry_ref, loc_ref, left_ref):
    group, depth = lax.axis_index("depth"), lax.axis_size("depth")
    nsrc = src_ref.shape[0] // 2
    rank = de_ref.shape[0] // 2
    rows = lax.broadcasted_iota(jnp.int32, (nsrc, list_ref.shape[1]), 0)
    cols = lax.broadcasted_iota(jnp.int32, (nsrc, list_ref.shape[1]), 1)
    hit = (rows == list_ref[...]) & (cols < count_ref[0])
    mask = jnp.sum(jnp.where(hit, 1.0, 0.0), axis=1, keepdims=True)
    local = src_ref[...] * jnp.concatenate([mask, mask], axis=0)
    loc_ref[...] = local
    eye = lax.broadcasted_iota(jnp.int32, (rank, rank), 0) == lax.broadcasted_iota(jnp.int32, (rank, rank), 1)
    for k, (basis_ref, decay_ref, edge) in enumerate(((de_ref, dd_ref, 0), (ue_ref, ud_ref, depth - 1))):
        decay = jnp.sum(jnp.where(eye, decay_ref[...], 0.0), axis=1, keepdims=True)
        basis = split(basis_ref[...] * jnp.concatenate([decay, decay], axis=0))
        first = jnp.where(group == edge, entry_ref[k * nsrc : (k + 1) * nsrc], 0.0)
        trace = split(local + dot3(split(spread(first)), basis, ROWS_COLS))
        for part in (0, 1):
            left_ref[k, part, : 2 * rank] = basis[part]
            left_ref[k, part, 2 * rank :] = trace[part]


def gram(which, proj_ref, left_ref):
    rank = proj_ref.shape[0] // 2
    out = dot3((left_ref[which, 0], left_ref[which, 1]), split(proj_ref[...]), ROWS_ROWS)
    return jnp.concatenate([joined(out[: 2 * rank]), joined(out[2 * rank :])], 0)


def first_gram_kernel(proj_ref, left_ref, out_ref):
    out_ref[...] = gram(1, proj_ref, left_ref)


def second_gram_kernel(proj_ref, left_ref, first_ref, keep_ref, give_ref):
    down, up = gram(0, proj_ref, left_ref), first_ref[...]
    ours = standing()[0] == 0
    keep_ref[...] = jnp.where(ours, down, up)
    give_ref[...] = jnp.where(ours, up, down)


def pair_kernel(count, *refs):
    parts, (near_ref, out_ref) = refs[:-2], refs[-2:]
    other = parts[0][...] + parts[2][...]
    own = parts[3][...] + parts[1][...]
    first = lax.rem(standing()[1], 2) == 0
    near = jnp.where(first, own, other)
    near_ref[...] = near
    out_ref[...] = compose(jnp.where(first, other, own), near)


def ordered(reach, own_ref, other_ref):
    own, other = own_ref[...], other_ref[...]
    lower = lax.rem(lax.div(standing()[1], reach), 2) == 0
    return jnp.where(lower, own, other), jnp.where(lower, other, own)


def total_kernel(reach, own_ref, other_ref, out_ref):
    earlier, later = ordered(reach, own_ref, other_ref)
    out_ref[...] = compose(later, earlier)


def gap_kernel(reach, own_ref, other_ref, out_ref):
    place = standing()[1]
    own, other = own_ref[...], other_ref[...]
    started = lax.rem(place, reach) >= 2
    upper = lax.rem(lax.div(place, reach), 2) == 1
    longer = jnp.where(started, compose(own, other), other)
    out_ref[...] = jnp.where(upper, longer, own)


def offset(step):
    return step[step.shape[1] // 2 :]


def final_kernel(quarter, order, *refs):
    parts, (near_ref, gap_ref, entry_ref, out_ref) = refs[:-4], refs[-4:]
    role, place = standing()
    mine = lax.div(place, quarter)
    totals = [parts[order.index(bits + 1)][...] for bits in range(len(order))]

    def earlier(k):
        chosen = totals[-1]
        for bits in range(len(totals) - 1, 0, -1):
            chosen = jnp.where(mine == (k ^ bits), totals[bits - 1], chosen)
        return chosen

    carry = jnp.where(mine > 0, offset(earlier(0)), 0.0)
    for k in range(1, len(totals)):
        carry = jnp.where(mine > k, advance(earlier(k), carry), carry)
    if quarter > 2:
        carry = jnp.where(lax.rem(place, quarter) >= 2, advance(gap_ref[...], carry), carry)
    carry = jnp.where(lax.rem(place, 2) == 1, advance(near_ref[...], carry), carry)
    nsrc = carry.shape[0]
    entry = jnp.where(role == 0, entry_ref[:nsrc], entry_ref[nsrc:])
    out_ref[...] = jnp.where(place == 0, entry, carry)


def expanded(turn, rows_ref, left_ref, sum_ref, columns):
    role = lax.rem(standing()[0] + turn, 2)
    wide = rows_ref.shape[1]
    basis = (left_ref[role, 0, :wide, columns], left_ref[role, 1, :wide, columns])
    return sum_ref[:, columns] + dot3(split(spread(rows_ref[...])), basis, ROWS_COLS)


def expand_kernel(rows_ref, left_ref, sum_ref, out_ref):
    out_ref[...] = expanded(0, rows_ref, left_ref, sum_ref, slice(None))


def finish_kernel(rows_ref, left_ref, sum_ref, out_ref, held_ref, done):
    width = held_ref.shape[1]
    copies = []
    for k, (start, stop) in enumerate(((0, width // 4), (width // 4, width))):
        columns = slice(start, stop)
        held_ref[:, columns] = expanded(1, rows_ref, left_ref, sum_ref, columns)
        copies.append(pltpu.make_async_copy(held_ref.at[:, columns], out_ref.at[:, columns], done.at[k]))
        copies[-1].start()
    for copy in copies:
        copy.wait()


def call(kernel, outs, *args, scalars=0, grant=4):
    return pl.pallas_call(
        kernel,
        out_shape=outs,
        in_specs=[SMEM] * scalars + [VMEM] * (len(args) - scalars),
        out_specs=jax.tree.map(lambda _: VMEM, outs),
        compiler_params=pltpu.CompilerParams(vmem_limit_bytes=grant << 20),
    )(*args)


def shape(*dims, dtype=F32):
    return jax.ShapeDtypeStruct(dims, dtype)


def body(
    sources,
    down_expand,
    down_project,
    up_expand,
    up_project,
    down_decay,
    up_decay,
    active_list,
    active_count,
    incident_down,
    incident_up,
):
    nsrc, width = sources.shape[2:]
    rank = down_expand.shape[2]
    depth, lat = lax.axis_size("depth"), lax.axis_size("lat")
    element = shape(rank + nsrc, 2 * rank)

    def flat(value):
        return value.reshape(value.shape[-3] * value.shape[-2], value.shape[-1])

    def shifted(value, step):
        return lax.ppermute(value, "depth", [(k, (k + step) % depth) for k in range(depth)])

    def swapped(value, deep, wide):
        pairs = [(g * lat + j, (g ^ deep) * lat + (j ^ wide)) for g in range(depth) for j in range(lat)]
        return lax.ppermute(value, ("depth", "lat"), pairs)

    def met(value, deep, wide):
        return swapped(value, deep, wide ^ parity(deep ^ wide))

    ahead = shifted(flat(down_project), -1)
    behind = shifted(flat(up_project), 1)

    entry = call(
        entry_kernel,
        shape(2 * nsrc, 2 * rank),
        flat(down_project),
        flat(up_project),
        flat(incident_down),
        flat(incident_up),
        grant=12,
    )
    bit = 1
    while bit < lat:
        entry = entry + swapped(entry, 0, bit)
        bit *= 2
    local, left = call(
        prepare_kernel,
        (shape(2 * nsrc, width), shape(2, 2, 2 * rank + 2 * nsrc, width, dtype=BF16)),
        active_count,
        active_list,
        flat(sources),
        flat(down_expand),
        flat(up_expand),
        down_decay,
        up_decay,
        entry,
        scalars=1,
        grant=12,
    )

    first = call(first_gram_kernel, element, behind, left)
    keep, give = call(second_gram_kernel, (element, element), ahead, left, first)
    own = keep + swapped(give, 0, 1)
    bit = 4
    while bit < lat:
        own = own + met(own, 0, bit)
        bit *= 2
    m = dict(xy=met(own, 1, 2), x=met(own, 0, 2), y=met(own, 1, 0), o=own)
    near, total = call(functools.partial(pair_kernel, 2), (element, element), *[m[k] for k in ['xy', 'x', 'y', 'o']])
    gap = near
    quarter = max(depth // 4, 2)
    reach = 2
    while reach < quarter:
        other = met(total, reach, 0)
        gap = other if reach == 2 else call(functools.partial(gap_kernel, reach), element, gap, other)
        total = call(functools.partial(total_kernel, reach), element, total, other)
        reach *= 2
    parts = []
    for bits in (2, 3, 1):
        if bits >= depth // quarter:
            continue
        moves = []
        for g in range(depth):
            for j in range(lat):
                up = parity(g ^ j) == 1
                place = depth - 1 - g if up else g
                deep = bits * quarter
                ahead_of = place < (place ^ deep)
                goal = (g ^ deep, j ^ parity(deep)) if ahead_of else (g, j ^ 1)
                moves.append((g * lat + j, goal[0] * lat + goal[1]))
        parts.append((bits, lax.ppermute(total, ("depth", "lat"), moves)))
    order = [bits for bits, _ in parts]
    coef = call(functools.partial(final_kernel, quarter, order), shape(nsrc, 2 * rank), *[part for _, part in parts], near, gap, entry)
    wide = shape(2 * nsrc, width)
    field = call(expand_kernel, wide, coef, left, local)
    field = pl.pallas_call(
        finish_kernel,
        out_shape=wide,
        in_specs=[VMEM] * 3,
        out_specs=pl.BlockSpec(memory_space=pl.ANY),
        scratch_shapes=[pltpu.VMEM(wide.shape, F32), pltpu.SemaphoreType.DMA((2,))],
        compiler_params=pltpu.CompilerParams(vmem_limit_bytes=4 << 20),
    )(swapped(coef, 0, 1), left, field)
    return field.reshape(sources.shape)


def solution(mesh):
    in_specs = (
        P("depth", None, None, "lat"),
        P("depth", None, None, "lat"),
        P("depth", None, None, "lat"),
        P("depth", None, None, "lat"),
        P("depth", None, None, "lat"),
        P("depth", None),
        P("depth", None),
        P("depth", None),
        P("depth"),
        P(None, None, "lat"),
        P(None, None, "lat"),
    )
    out_specs = P("depth", None, None, "lat")
    return jax.shard_map(body, mesh=mesh, in_specs=in_specs, out_specs=out_specs, check_vma=False)
```

```python
import functools

import jax
import jax.numpy as jnp
from jax import lax
from jax.experimental import pallas as pl
from jax.experimental.pallas import tpu as pltpu
from jax.sharding import PartitionSpec as P

F32 = jnp.float32
BF16 = jnp.bfloat16
VMEM = pl.BlockSpec(memory_space=pltpu.VMEM)
SMEM = pl.BlockSpec(memory_space=pltpu.SMEM)


def split(value):
    high = value.astype(BF16)
    return high, (value - high.astype(F32)).astype(BF16)


ROWS_COLS = ((1,), (0,))
ROWS_ROWS = ((1,), (1,))


def dot3(left, right, dims):
    def prod(a, b):
        return lax.dot_general(a, b, (dims, ((), ())), preferred_element_type=F32)

    if dims == ROWS_COLS:
        return prod(jnp.concatenate([left[0], left[0], left[1]], 1), jnp.concatenate([right[0], right[1], right[0]], 0))
    count = right[0].shape[0]
    both = prod(left[0], jnp.concatenate(right, 0))
    return both[:, :count] + (both[:, count:] + prod(left[1], right[0]))


def turned(value):
    half = value.shape[1] // 2
    lanes = lax.broadcasted_iota(jnp.int32, value.shape, 1)
    swapped = pltpu.roll(value, half, 1)
    return jnp.where(lanes < half, -swapped, swapped)


def joined(product):
    half = product.shape[0] // 2
    return product[:half] + turned(product[half:])


def spread(rows):
    half = rows.shape[1] // 2
    lanes = lax.broadcasted_iota(jnp.int32, rows.shape, 1)
    return jnp.concatenate([jnp.where(lanes < half, rows, -rows), pltpu.roll(rows, half, 1)], axis=0)


def apply_map(rows, step):
    rank = step.shape[1] // 2
    matrix = step[:rank]
    full = jnp.concatenate([matrix, turned(matrix)], axis=0)
    return dot3(split(rows), split(full), ROWS_COLS)


def compose(later, earlier):
    rank = later.shape[1] // 2
    out = apply_map(earlier, later)
    return jnp.concatenate([out[:rank], out[rank:] + later[rank:]], axis=0)


def advance(step, rows):
    rank = step.shape[1] // 2
    return apply_map(rows, step) + step[rank:]


def parity(value):
    odd = value & 1
    for bit in range(1, 16):
        odd = odd ^ ((value >> bit) & 1)
    return odd


def standing():
    group, depth = lax.axis_index("depth"), lax.axis_size("depth")
    role = parity(group ^ lax.axis_index("lat"))
    return role, jnp.where(role == 0, group, depth - 1 - group)


def entry_kernel(dp_ref, up_ref, di_ref, ui_ref, out_ref):
    for k, (proj, wave) in enumerate(((dp_ref, di_ref), (up_ref, ui_ref))):
        half = wave.shape[0] // 2
        out = dot3(split(wave[...]), split(proj[...]), ROWS_ROWS)
        out_ref[k * half : (k + 1) * half] = joined(out)


def prepare_kernel(count_ref, list_ref, src_ref, de_ref, ue_ref, dd_ref, ud_ref, entry_ref, loc_ref, left_ref):
    group, depth = lax.axis_index("depth"), lax.axis_size("depth")
    nsrc = src_ref.shape[0] // 2
    rank = de_ref.shape[0] // 2
    rows = lax.broadcasted_iota(jnp.int32, (nsrc, list_ref.shape[1]), 0)
    cols = lax.broadcasted_iota(jnp.int32, (nsrc, list_ref.shape[1]), 1)
    hit = (rows == list_ref[...]) & (cols < count_ref[0])
    mask = jnp.sum(jnp.where(hit, 1.0, 0.0), axis=1, keepdims=True)
    local = src_ref[...] * jnp.concatenate([mask, mask], axis=0)
    loc_ref[...] = local
    eye = lax.broadcasted_iota(jnp.int32, (rank, rank), 0) == lax.broadcasted_iota(jnp.int32, (rank, rank), 1)
    for k, (basis_ref, decay_ref, edge) in enumerate(((de_ref, dd_ref, 0), (ue_ref, ud_ref, depth - 1))):
        decay = jnp.sum(jnp.where(eye, decay_ref[...], 0.0), axis=1, keepdims=True)
        basis = split(basis_ref[...] * jnp.concatenate([decay, decay], axis=0))
        first = jnp.where(group == edge, entry_ref[k * nsrc : (k + 1) * nsrc], 0.0)
        trace = split(local + dot3(split(spread(first)), basis, ROWS_COLS))
        for part in (0, 1):
            left_ref[k, part, : 2 * rank] = basis[part]
            left_ref[k, part, 2 * rank :] = trace[part]


def gram(which, proj_ref, left_ref):
    rank = proj_ref.shape[0] // 2
    out = dot3((left_ref[which, 0], left_ref[which, 1]), split(proj_ref[...]), ROWS_ROWS)
    return jnp.concatenate([joined(out[: 2 * rank]), joined(out[2 * rank :])], 0)


def first_gram_kernel(proj_ref, left_ref, out_ref):
    out_ref[...] = gram(1, proj_ref, left_ref)


def second_gram_kernel(proj_ref, left_ref, first_ref, keep_ref, give_ref):
    down, up = gram(0, proj_ref, left_ref), first_ref[...]
    ours = standing()[0] == 0
    keep_ref[...] = jnp.where(ours, down, up)
    give_ref[...] = jnp.where(ours, up, down)


def pair_kernel(*refs):
    parts, (near_ref, out_ref) = refs[:-2], refs[-2:]
    other, own = parts[0][...], parts[1][...]
    for other_ref, own_ref in zip(parts[2::2], parts[3::2]):
        other, own = other + other_ref[...], own + own_ref[...]
    first = lax.rem(standing()[1], 2) == 0
    near = jnp.where(first, own, other)
    near_ref[...] = near
    out_ref[...] = compose(jnp.where(first, other, own), near)


def ordered(reach, own_ref, other_ref):
    own, other = own_ref[...], other_ref[...]
    lower = lax.rem(lax.div(standing()[1], reach), 2) == 0
    return jnp.where(lower, own, other), jnp.where(lower, other, own)


def total_kernel(reach, own_ref, other_ref, out_ref):
    earlier, later = ordered(reach, own_ref, other_ref)
    out_ref[...] = compose(later, earlier)


def gap_kernel(reach, own_ref, other_ref, out_ref):
    place = standing()[1]
    own, other = own_ref[...], other_ref[...]
    started = lax.rem(place, reach) >= 2
    upper = lax.rem(lax.div(place, reach), 2) == 1
    longer = jnp.where(started, compose(own, other), other)
    out_ref[...] = jnp.where(upper, longer, own)


def offset(step):
    return step[step.shape[1] // 2 :]


def final_kernel(quarter, order, *refs):
    parts, (near_ref, gap_ref, entry_ref, out_ref) = refs[:-4], refs[-4:]
    role, place = standing()
    mine = lax.div(place, quarter)
    totals = [parts[order.index(bits + 1)][...] for bits in range(len(order))]

    def earlier(k):
        chosen = totals[-1]
        for bits in range(len(totals) - 1, 0, -1):
            chosen = jnp.where(mine == (k ^ bits), totals[bits - 1], chosen)
        return chosen

    carry = jnp.where(mine > 0, offset(earlier(0)), 0.0)
    for k in range(1, len(totals)):
        carry = jnp.where(mine > k, advance(earlier(k), carry), carry)
    if quarter > 2:
        carry = jnp.where(lax.rem(place, quarter) >= 2, advance(gap_ref[...], carry), carry)
    carry = jnp.where(lax.rem(place, 2) == 1, advance(near_ref[...], carry), carry)
    nsrc = carry.shape[0]
    entry = jnp.where(role == 0, entry_ref[:nsrc], entry_ref[nsrc:])
    out_ref[...] = jnp.where(place == 0, entry, carry)


def expanded(turn, rows_ref, left_ref, sum_ref, columns):
    role = lax.rem(standing()[0] + turn, 2)
    wide = rows_ref.shape[1]
    basis = (left_ref[role, 0, :wide, columns], left_ref[role, 1, :wide, columns])
    return sum_ref[:, columns] + dot3(split(spread(rows_ref[...])), basis, ROWS_COLS)


def expand_kernel(rows_ref, left_ref, sum_ref, out_ref):
    out_ref[...] = expanded(0, rows_ref, left_ref, sum_ref, slice(None))


def finish_kernel(rows_ref, left_ref, sum_ref, out_ref, held_ref, done):
    width = held_ref.shape[1]
    copies = []
    for k, (start, stop) in enumerate(((0, width // 4), (width // 4, width))):
        columns = slice(start, stop)
        held_ref[:, columns] = expanded(1, rows_ref, left_ref, sum_ref, columns)
        copies.append(pltpu.make_async_copy(held_ref.at[:, columns], out_ref.at[:, columns], done.at[k]))
        copies[-1].start()
    for copy in copies:
        copy.wait()


def call(kernel, outs, *args, scalars=0, grant=4):
    return pl.pallas_call(
        kernel,
        out_shape=outs,
        in_specs=[SMEM] * scalars + [VMEM] * (len(args) - scalars),
        out_specs=jax.tree.map(lambda _: VMEM, outs),
        compiler_params=pltpu.CompilerParams(vmem_limit_bytes=grant << 20),
    )(*args)


def shape(*dims, dtype=F32):
    return jax.ShapeDtypeStruct(dims, dtype)


def body(
    sources,
    down_expand,
    down_project,
    up_expand,
    up_project,
    down_decay,
    up_decay,
    active_list,
    active_count,
    incident_down,
    incident_up,
):
    nsrc, width = sources.shape[2:]
    rank = down_expand.shape[2]
    depth, lat = lax.axis_size("depth"), lax.axis_size("lat")
    element = shape(rank + nsrc, 2 * rank)

    def flat(value):
        return value.reshape(value.shape[-3] * value.shape[-2], value.shape[-1])

    def shifted(value, step):
        return lax.ppermute(value, "depth", [(k, (k + step) % depth) for k in range(depth)])

    def swapped(value, deep, wide):
        pairs = [(g * lat + j, (g ^ deep) * lat + (j ^ wide)) for g in range(depth) for j in range(lat)]
        return lax.ppermute(value, ("depth", "lat"), pairs)

    def met(value, deep, wide):
        return swapped(value, deep, wide ^ parity(deep ^ wide))

    ahead = shifted(flat(down_project), -1)
    behind = shifted(flat(up_project), 1)

    entry = call(
        entry_kernel,
        shape(2 * nsrc, 2 * rank),
        flat(down_project),
        flat(up_project),
        flat(incident_down),
        flat(incident_up),
        grant=12,
    )
    bit = 1
    while bit < lat:
        entry = entry + swapped(entry, 0, bit)
        bit *= 2
    local, left = call(
        prepare_kernel,
        (shape(2 * nsrc, width), shape(2, 2, 2 * rank + 2 * nsrc, width, dtype=BF16)),
        active_count,
        active_list,
        flat(sources),
        flat(down_expand),
        flat(up_expand),
        down_decay,
        up_decay,
        entry,
        scalars=1,
        grant=12,
    )

    first = call(first_gram_kernel, element, behind, left)
    keep, give = call(second_gram_kernel, (element, element), ahead, left, first)
    own = keep + swapped(give, 0, 1)
    bit = 4
    while bit < lat:
        own = own + met(own, 0, bit)
        bit *= 2
    if lat > 2:
        others, owns = [met(own, 1, 2)], [met(own, 0, 2), own]
        others.append(met(own, 1, 0))
        parts = [others[0], owns[0], others[1], owns[1]]
    else:
        parts = [met(own, 1, 0), own]
    near, total = call(pair_kernel, (element, element), *parts)
    gap = near
    quarter = max(depth // 4, 2)
    reach = 2
    while reach < quarter:
        other = met(total, reach, 0)
        gap = other if reach == 2 else call(functools.partial(gap_kernel, reach), element, gap, other)
        total = call(functools.partial(total_kernel, reach), element, total, other)
        reach *= 2
    parts = []
    for bits in (2, 3, 1):
        if bits >= depth // quarter:
            continue
        moves = []
        for g in range(depth):
            for j in range(lat):
                up = parity(g ^ j) == 1
                place = depth - 1 - g if up else g
                deep = bits * quarter
                ahead_of = place < (place ^ deep)
                goal = (g ^ deep, j ^ parity(deep)) if ahead_of else (g, j ^ 1)
                moves.append((g * lat + j, goal[0] * lat + goal[1]))
        parts.append((bits, lax.ppermute(total, ("depth", "lat"), moves)))
    order = [bits for bits, _ in parts]
    coef = call(functools.partial(final_kernel, quarter, order), shape(nsrc, 2 * rank), *[part for _, part in parts], near, gap, entry)
    wide = shape(2 * nsrc, width)
    field = call(expand_kernel, wide, coef, left, local)
    field = pl.pallas_call(
        finish_kernel,
        out_shape=wide,
        in_specs=[VMEM] * 3,
        out_specs=pl.BlockSpec(memory_space=pl.ANY),
        scratch_shapes=[pltpu.VMEM(wide.shape, F32), pltpu.SemaphoreType.DMA((2,))],
        compiler_params=pltpu.CompilerParams(vmem_limit_bytes=4 << 20),
    )(swapped(coef, 0, 1), left, field)
    return field.reshape(sources.shape)


def solution(mesh):
    in_specs = (
        P("depth", None, None, "lat"),
        P("depth", None, None, "lat"),
        P("depth", None, None, "lat"),
        P("depth", None, None, "lat"),
        P("depth", None, None, "lat"),
        P("depth", None),
        P("depth", None),
        P("depth", None),
        P("depth"),
        P(None, None, "lat"),
        P(None, None, "lat"),
    )
    out_specs = P("depth", None, None, "lat")
    return jax.shard_map(body, mesh=mesh, in_specs=in_specs, out_specs=out_specs, check_vma=False)
```
